32 devices in a mesh: dom: 8 (over z, y), grp: 4 (over x, core).
Axes of the slice: x: 2, y: 2, z: 4, core: 2. Of those that a mesh axis runs over, the one named last changes fastest.
Arguments:
- profile: bfloat16 [768, 2, 64, 128], P(('dom', 'grp')), may hold values from -6 to 6
- forcing: bfloat16 [768, 2, 128], P(('dom', 'grp')), may hold values from -6 to 6
- height: bfloat16 [768, 128], P(('dom', 'grp')), may hold values from 0.5 to 2
- area: float32 [768, 128], P(('dom', 'grp')), may hold values from 0.5 to 2
- stretch: int32 [768], P(('dom', 'grp')), may hold values from 0 to 3
- face_cell: int32 [768, 128], P(('dom', 'grp')), may hold values from 0 to 127
- match_owner: int32 [8, 4, 24], P(None, 'grp'), may hold values from 0 to 7, as said below
- match_block: int32 [8, 4, 24], P(None, 'grp'), may hold values from 0 to 11
- live_blocks: int32 [32], replicated, may hold values from 6 to 24, as said below
- cell_velocity: bfloat16 [384, 2, 128], P(('dom', 'grp')), may hold values from -6 to 6
Outputs:
- wall_shear: float32 [768, 2, 128], P(('dom', 'grp'))
- wall_force: float32 [384, 2, 128], P(('dom', 'grp'))
The draws below stay inside these ranges and needn't reach their ends.
Inputs may be any that keep to these rules, and one draw needn't show every extreme that they name: `match_owner`: of the blocks of one device, at most 6 have the same owner, and in every device one owner has exactly 6. The first live_blocks blocks of a device hold faces. Among the devices of one dom index, exactly one has all 24 blocks in use.
All inputs are finite; a program needn't handle non-finite values.
Results may differ from the reference program's by a relative error of at most 0.001.
Values may be sent and summed in bfloat16 or wider, within the bound.
A program may use at most 64 MiB of HBM per device.

```python
import math
import jax
import jax.numpy as jnp
from jax import lax

NP = 64
FB = 128
BLK_DEV = 24
STEPS = 4
CBLK = 12
CAP = 6
FACEB = 768
CELLB = 384
N_DOM = 8
N_GRP = 4


def draw_match_owner(key, part):
    device_keys = jax.random.split(jax.random.fold_in(key, 7), N_DOM * N_GRP)

    def one_device(device_key):
        special_key, spread_key, place_key = jax.random.split(device_key, 3)
        special = jax.random.randint(special_key, (), 0, N_DOM, dtype=jnp.int32)
        others = jnp.arange((N_DOM - 1) * CAP, dtype=jnp.int32) // CAP
        others = others + (others >= special).astype(jnp.int32)
        picked = jax.random.permutation(spread_key, others)[:BLK_DEV - CAP]
        owner_table = jnp.concatenate([jnp.full((CAP,), special, dtype=jnp.int32), picked])
        return jax.random.permutation(place_key, owner_table)
    return jax.vmap(one_device)(device_keys).reshape(N_DOM, N_GRP, BLK_DEV).astype(jnp.int32)


def draw_live_blocks(key, part):
    base_key, full_key = jax.random.split(jax.random.fold_in(key, 11))
    counts = jax.random.randint(base_key, (N_DOM, N_GRP), BLK_DEV // 4, 7 * BLK_DEV // 8 + 1, dtype=jnp.int32)
    fullest = jax.random.randint(full_key, (N_DOM,), 0, N_GRP, dtype=jnp.int32)
    counts = jnp.where(jnp.arange(N_GRP, dtype=jnp.int32)[None, :] == fullest[:, None], BLK_DEV, counts)
    return counts.reshape(-1).astype(jnp.int32)


def set_ends(entries, own_key, least, largest):
    spot = [jax.random.randint(jax.random.fold_in(own_key, axis), (), 0, length) for axis, length in enumerate(entries.shape)]
    main_axis = entries.shape.index(max(entries.shape))
    neighbour = spot[:main_axis] + [(spot[main_axis] + 1) % entries.shape[main_axis]] + spot[main_axis + 1:]
    return entries.at[tuple(spot)].set(least).at[tuple(neighbour)].set(largest)


def level_of(own_key, shape, cuts, smallest, high):
    gain, own = 1.0, jax.random.fold_in(own_key, 6)
    for dim, blocks in cuts:
        steps = jnp.exp(jax.random.uniform(jax.random.fold_in(own, dim), (blocks,), jnp.float32, smallest / len(cuts), high / len(cuts)))
        gain = gain * jnp.repeat(steps, shape[dim] // blocks).reshape([-1 if axis == dim else 1 for axis in range(len(shape))])
    return gain


def noise(own_key, extent, scale, reach, shards=(), held_as=jnp.bfloat16):
    drawn = scale * jax.random.normal(own_key, extent, jnp.float32)
    if shards:
        drawn = drawn * level_of(own_key, extent, shards, -0.22, 0.18)
    return jnp.clip(drawn, -reach, reach).astype(held_as)


def setup_inputs(seed: int = 0) -> dict:
    key_list = jax.random.split(jax.random.key(seed), 11)
    profile = noise(key_list[0], (FACEB, 2, NP, FB), 1.0, 6.0, ((0, 32),))
    forcing = noise(key_list[1], (FACEB, 2, FB), 1.0, 6.0, ((0, 32),))
    height = jnp.clip(jnp.exp(math.log(2.0) - 1.3862944 * jax.random.uniform(key_list[2], (FACEB, FB), jnp.float32) ** level_of(key_list[2], (FACEB, FB), ((0, 32),), -0.2, 0.2)), 0.5, 2.0).astype(jnp.bfloat16)
    area = jnp.clip(jnp.exp(math.log(2.0) - 1.3862944 * jax.random.uniform(key_list[3], (FACEB, FB), jnp.float32) ** level_of(key_list[3], (FACEB, FB), ((0, 32),), -0.2, 0.2)), 0.5, 2.0)
    stretch = set_ends(jax.random.randint(key_list[4], (FACEB,), 0, 4), jax.random.fold_in(key_list[4], 1), 0, 3).astype(jnp.int32)
    face_cell = set_ends(jax.random.randint(key_list[5], (FACEB, FB), 0, FB), jax.random.fold_in(key_list[5], 1), 0, FB - 1).astype(jnp.int32)
    match_owner = draw_match_owner(jax.random.fold_in(key_list[10], 71), 0)
    match_block = set_ends(jax.random.randint(key_list[7], (N_DOM, N_GRP, BLK_DEV), 0, CBLK), jax.random.fold_in(key_list[7], 1), 0, CBLK - 1).astype(jnp.int32)
    live_blocks = draw_live_blocks(jax.random.fold_in(key_list[10], 71), 0)
    cell_velocity = noise(key_list[9], (CELLB, 2, FB), 1.0, 6.0, ((0, 32),))
    return {"profile": profile, "forcing": forcing, "height": height, "area": area, "stretch": stretch, "face_cell": face_cell, "match_owner": match_owner, "match_block": match_block, "live_blocks": live_blocks, "cell_velocity": cell_velocity}


VISCOSITY = 0.005
KARMAN = 0.41
TIME_STEP = 2.0
PUSH_GAIN = 0.5
BASE_RATE = 1.5

def wall_grid(height, stretch, points):
    levels = jnp.arange(points + 1, dtype=jnp.float32) / points
    stretch_rate = BASE_RATE + stretch.astype(jnp.float32)
    growth = jnp.exp(stretch_rate[:, None] * levels[None, :]) - 1.0
    fraction = growth / growth[:, -1:]
    depths = fraction[:, :, None] * height.astype(jnp.float32)[:, None, :]
    spacing = depths[:, 1:] - depths[:, :-1]
    middle = 0.5 * (depths[:, 1:] + depths[:, :-1])
    return (spacing, middle)

def viscosity(profile_now, spacing, middle):
    below_point = jnp.concatenate([jnp.zeros_like(profile_now[:, :, :1]), profile_now[:, :, :-1]], axis=2)
    increment = profile_now - below_point
    strain = jnp.sqrt(increment[:, 0] ** 2 + increment[:, 1] ** 2) / spacing
    return VISCOSITY + (KARMAN * middle) ** 2 * strain

def thomas_solve(lower_band, diagonal, upper_band, right_side):
    points = diagonal.shape[1]
    factor_list = []
    value_list = []
    denom = diagonal[:, 0]
    factor_now = upper_band[:, 0] / denom
    value_now = right_side[:, :, 0] / denom[:, None]
    factor_list.append(factor_now)
    value_list.append(value_now)
    for level in range(1, points):
        lower_now = lower_band[:, level]
        denom = diagonal[:, level] - lower_now * factor_now
        factor_now = upper_band[:, level] / denom
        value_now = (right_side[:, :, level] - lower_now[:, None] * value_now) / denom[:, None]
        factor_list.append(factor_now)
        value_list.append(value_now)
    answer = [None] * points
    answer[points - 1] = value_list[points - 1]
    for level in range(points - 2, -1, -1):
        answer[level] = value_list[level] - factor_list[level][:, None] * answer[level + 1]
    return jnp.stack(answer, axis=2)

def implicit_step(profile_now, source, matching, spacing, middle):
    points = spacing.shape[1]
    mixing = viscosity(profile_now, spacing, middle)
    upper_mix = jnp.concatenate([mixing[:, 1:], mixing[:, -1:]], axis=1)
    upper_gap = jnp.concatenate([spacing[:, 1:], spacing[:, -1:]], axis=1)
    centre = 0.5 * (spacing + upper_gap)
    down_coef = TIME_STEP * mixing / (spacing * centre)
    up_coef = TIME_STEP * upper_mix / (upper_gap * centre)
    row_index = lax.broadcasted_iota(jnp.int32, spacing.shape, 1)
    last_row = row_index == points - 1
    lower_band = jnp.where((row_index == 0) | last_row, 0.0, -down_coef)
    upper_band = jnp.where(last_row, 0.0, -up_coef)
    diagonal = jnp.where(last_row, 1.0, 1.0 + down_coef + up_coef)
    right_side = jnp.where(last_row[:, None], matching[:, :, None, :], profile_now + TIME_STEP * source[:, :, None, :])
    return thomas_solve(lower_band, diagonal, upper_band, right_side)

def wall_shear_of(profile_in, forcing, matching, height, stretch):
    points = profile_in.shape[2]
    spacing, middle = wall_grid(height, stretch, points)
    start_profile = profile_in.astype(jnp.float32)
    matching = matching.astype(jnp.float32)
    source = PUSH_GAIN * (forcing.astype(jnp.float32) + matching - start_profile[:, :, -1, :])
    profile_now = jnp.concatenate([start_profile[:, :, :-1], matching[:, :, None, :]], axis=2)
    for inner_step in range(STEPS):
        profile_now = implicit_step(profile_now, source, matching, spacing, middle)
    mixing = viscosity(profile_now, spacing, middle)
    return (mixing[:, 0] / spacing[:, 0])[:, None, :] * profile_now[:, :, 0]

def reference(profile, forcing, height, area, stretch, face_cell, match_owner, match_block, live_blocks, cell_velocity):
    device_total = N_DOM * N_GRP
    columns = jnp.arange(N_GRP, dtype=jnp.int32)[None, :, None]
    global_block = ((match_owner * N_GRP + columns) * CBLK + match_block).reshape(-1).astype(jnp.int32)
    slot_rows = jnp.take(cell_velocity, global_block, axis=0)
    index_grid = jnp.broadcast_to(face_cell[:, None, :], slot_rows.shape).astype(jnp.int32)
    matching = jnp.take_along_axis(slot_rows, index_grid, axis=2)
    live_mask = (jnp.arange(BLK_DEV, dtype=jnp.int32)[None, :] < live_blocks[:, None]).reshape(-1)

    def per_device(pieces):
        return wall_shear_of(pieces[0], pieces[1], pieces[2], pieces[3], pieces[4])
    shear_all = lax.map(per_device, (profile.reshape(device_total, BLK_DEV, 2, NP, FB), forcing.reshape(device_total, BLK_DEV, 2, FB), matching.reshape(device_total, BLK_DEV, 2, FB), height.reshape(device_total, BLK_DEV, FB), stretch.reshape(device_total, BLK_DEV)))
    shear_all = jnp.where(live_mask[:, None, None], shear_all.reshape(FACEB, 2, FB), 0.0)
    contrib = shear_all * area[:, None, :]
    cell_index = (global_block[:, None] * FB + face_cell).reshape(-1).astype(jnp.int32)
    face_terms = jnp.transpose(contrib, (0, 2, 1)).reshape(-1, 2)
    cell_force = jax.ops.segment_sum(face_terms, cell_index, num_segments=CELLB * FB)
    cell_force = jnp.transpose(cell_force.reshape(CELLB, FB, 2), (0, 2, 1))
    return (shear_all, cell_force)
```

```python
import functools

import jax
import jax.numpy as jnp
from jax import lax
from jax.experimental import pallas as pl
from jax.experimental.pallas import tpu as pltpu
from jax.sharding import PartitionSpec as P

STEPS = 4
VISCOSITY = 0.005
KARMAN = 0.41
TIME_STEP = 2.0
PUSH_GAIN = 0.5
BASE_RATE = 1.5
MESH = pl.DeviceIdType.MESH
F32 = jnp.float32
BF16 = jnp.bfloat16


def kernel(
    doms,
    grps,
    prof_h,
    forc_h,
    height_h,
    area_h,
    stretch_h,
    face_h,
    owner_h,
    target_h,
    live_h,
    cell_h,
    shear_ref,
    force_ref,
    prof,
    forc,
    height,
    area,
    stretch,
    face,
    owner,
    target,
    live,
    table,
    stage,
    u,
    gval,
    fac,
    base,
    quad,
    gap,
    pick,
    cells,
    packed,
    arrived,
    in_sem,
    own_sem,
    cell_send,
    cell_recv,
    force_send,
    force_recv,
):
    blocks, _, points, faces = prof.shape
    rows = cell_h.shape[0]
    me = lax.axis_index("dom")
    mine = lax.axis_index("grp")
    wide = (blocks, faces)

    barrier = pltpu.get_barrier_semaphore()
    for j in range(1, doms):
        pl.semaphore_signal(
            barrier, inc=1, device_id={"dom": lax.rem(me + j, doms)}, device_id_type=MESH
        )
    loads = []
    for i, (src, dst) in enumerate(
        (
            (stretch_h, stretch),
            (height_h, height),
            (owner_h, owner),
            (target_h, target),
            (face_h, face),
            (prof_h, prof),
            (forc_h, forc),
            (area_h, area),
            (live_h, live),
        )
    ):
        loads.append(pltpu.make_async_copy(src, dst, in_sem.at[i]))
        loads[-1].start()
    own = pltpu.make_async_copy(cell_h, table.at[me], own_sem)
    own.start()
    pl.semaphore_wait(barrier, doms - 1)
    cell_copies = []
    for j in range(1, doms):
        cell_copies.append(
            pltpu.make_async_remote_copy(
                src_ref=cell_h,
                dst_ref=table.at[me],
                send_sem=cell_send.at[j],
                recv_sem=cell_recv.at[j],
                device_id={"dom": lax.rem(me + j, doms)},
                device_id_type=MESH,
            )
        )
        cell_copies[-1].start()
    for load in loads:
        load.wait()

    eye = lax.broadcasted_iota(jnp.int32, (blocks, blocks), 0) == lax.broadcasted_iota(
        jnp.int32, (blocks, blocks), 1
    )

    def as_column(row):
        spread = jnp.broadcast_to(row.astype(F32), (blocks, blocks))
        return jnp.sum(jnp.where(eye, spread, 0.0), axis=1, keepdims=True)

    rate = BASE_RATE + as_column(stretch[...])
    tall = height[...].astype(F32)
    step_rate = jnp.broadcast_to(rate / points, wide)
    growth = jnp.exp(step_rate)
    first = (growth - 1.0) / (jnp.exp(jnp.broadcast_to(rate, wide)) - 1.0)
    base_scale = TIME_STEP * VISCOSITY / (first * tall)
    gap_scale = 0.5 * tall * first * (1.0 + growth)
    mid_scale = 1.0 / (growth - 1.0)
    mid_first = 0.5 * (1.0 + growth)

    def grid_level(m, carry):
        level = m.astype(F32)
        shrink = jnp.exp(-step_rate * level)
        base[m] = base_scale * shrink
        ratio = KARMAN * (mid_first - shrink) * mid_scale
        quad[m] = TIME_STEP * ratio * ratio
        gap[m] = gap_scale * jnp.exp(step_rate * (level - 1.0))
        return carry

    lax.fori_loop(0, points, grid_level, 0)

    def widen(b, carry):
        stage[pl.ds(pl.multiple_of(b * 2 * points, 2 * points), 2 * points), :] = (
            prof[b].astype(F32).reshape(2 * points, faces)
        )
        return carry

    lax.fori_loop(0, blocks, widen, 0)

    def turn(k, carry):
        for c in range(2):
            u[k, c] = stage[pl.ds(c * points + k, blocks, stride=2 * points), :]
        return carry

    lax.fori_loop(0, points, turn, 0)

    face_now = face[...]
    cell_ids = lax.broadcasted_iota(jnp.int32, (faces, faces), 0)

    for b in range(blocks):
        pick[b] = (cell_ids == face_now[b : b + 1, :]).astype(F32).astype(BF16)

    row_global = owner[me] * rows + 2 * target[me]
    col_global = as_column(row_global).astype(jnp.int32)
    slots = doms * rows
    slot_lane = lax.broadcasted_iota(jnp.int32, (blocks, slots), 1)
    choose = jnp.concatenate(
        [(slot_lane == col_global + c).astype(F32) for c in range(2)], axis=0
    ).astype(BF16)

    own.wait()
    for copy in cell_copies:
        copy.wait()

    held = table[...].astype(F32).reshape(slots, faces).astype(BF16)
    slot_rows = jnp.dot(choose, held, preferred_element_type=F32)
    matching = [
        jnp.take_along_axis(
            slot_rows[c * blocks : (c + 1) * blocks], face_now, axis=1, mode="promise_in_bounds"
        )
        for c in range(2)
    ]
    source = []
    for c in range(2):
        push = forc[pl.ds(c, blocks, stride=2), :] + matching[c] - u[points - 1, c]
        source.append(TIME_STEP * PUSH_GAIN * push)
        u[points - 1, c] = matching[c]

    def flux(m, low, high):
        d0 = high[0] - low[0]
        d1 = high[1] - low[1]
        square = d0 * d0 + d1 * d1
        root = square * lax.rsqrt(jnp.maximum(square, 1e-37))
        return base[m] + quad[m] * root

    def point(k):
        return (u[k - 1, 0], u[k - 1, 1])

    zero = jnp.zeros(wide, F32)
    half = points // 2

    def eliminate(k, e, g, near, far, here):
        h = gap[k]
        p = h + near * e
        r = 1.0 / (p + far)
        e_new = p * r
        f_new = far * r
        g_new = tuple((h * (here[c] + source[c]) + near * g[c]) * r for c in range(2))
        return e_new, f_new, g_new

    def time_step(_, carry):
        below = point(1)
        low_flux = flux(0, (zero, zero), below)
        low_e, low_g = jnp.ones(wide, F32), (zero, zero)
        above = point(points - 1)
        edge = point(points)
        high_flux = flux(points - 1, above, edge)
        high_e, high_g = jnp.ones(wide, F32), edge
        for i in range(half):
            k = i + 1
            after = point(k + 1)
            next_flux = flux(k, below, after)
            low_e, low_f, low_g = eliminate(k, low_e, low_g, low_flux, next_flux, below)
            if i < half - 1:
                fac[k] = low_f
                for c in range(2):
                    gval[k, c] = low_g[c]
            low_flux, below = next_flux, after
            k = points - 1 - i
            if k > half:
                after = point(k - 1)
                next_flux = flux(k - 1, after, above)
                high_e, high_f, high_g = eliminate(
                    k, high_e, high_g, high_flux, next_flux, above
                )
                if k > half + 1:
                    fac[k] = high_f
                    for c in range(2):
                        gval[k, c] = high_g[c]
                high_flux, above = next_flux, after
        share = 1.0 / (low_e + low_f * high_e)
        down = [(low_g[c] + low_f * high_g[c]) * share for c in range(2)]
        up = [high_g[c] + high_f * down[c] for c in range(2)]
        for c in range(2):
            u[half - 1, c] = down[c]
            u[half, c] = up[c]
        for i in range(1, half):
            k = half - i
            f = fac[k]
            for c in range(2):
                down[c] = gval[k, c] + f * down[c]
                u[k - 1, c] = down[c]
            k = half + 1 + i
            if k < points:
                f = fac[k]
                for c in range(2):
                    up[c] = gval[k, c] + f * up[c]
                    u[k - 1, c] = up[c]
        return carry

    lax.fori_loop(0, STEPS, time_step, 0)

    wall = point(1)
    wall_flux = flux(0, (zero, zero), wall) * (1.0 / TIME_STEP)
    lane = lax.broadcasted_iota(jnp.int32, live.shape, 1)
    own_live = jnp.sum(
        jnp.where(lane == me * grps + mine, live[...], 0).astype(F32), axis=1, keepdims=True
    )
    alive = lax.broadcasted_iota(jnp.int32, wide, 0).astype(F32) < own_live
    size = area[...]
    pieces = []
    for c in range(2):
        shear = jnp.where(alive, wall_flux * wall[c], 0.0)
        shear_ref[pl.ds(c, blocks, stride=2), :] = shear
        pieces.append(shear * size)
    for c in range(2):
        top = pieces[c].astype(BF16).astype(F32)
        cells[pl.ds(c, blocks, stride=8), :] = top
        cells[pl.ds(2 + c, blocks, stride=8), :] = pieces[c] - top
    for c in range(4):
        cells[pl.ds(4 + c, blocks, stride=8), :] = zero
    for b in range(blocks):
        part = cells[pl.ds(8 * b, 8), :].astype(BF16)
        cells[pl.ds(8 * b, 8), :] = lax.dot_general(
            part, pick[b], (((1,), (1,)), ((), ())), preferred_element_type=F32
        )
    slot_row = lax.broadcasted_iota(jnp.int32, (slots, blocks), 0)
    total = jnp.zeros((slots, faces), F32)
    for c in range(2):
        by_cell = cells[pl.ds(c, blocks, stride=8), :] + cells[pl.ds(2 + c, blocks, stride=8), :]
        place = (slot_row == row_global + c).astype(F32)
        total += jnp.dot(
            place, by_cell, precision=lax.Precision.HIGHEST, preferred_element_type=F32
        )
    packed[...] = total.reshape(doms, rows, faces)
    force_copies = []
    for j in range(1, doms):
        peer = lax.rem(me + j, doms)
        force_copies.append(
            pltpu.make_async_remote_copy(
                src_ref=packed.at[peer],
                dst_ref=arrived.at[j],
                send_sem=force_send.at[j],
                recv_sem=force_recv.at[j],
                device_id={"dom": peer},
                device_id_type=MESH,
            )
        )
        force_copies[-1].start()
    result = packed[me]
    for j in range(1, doms):
        force_copies[j - 1].wait_recv()
        result += arrived[j]
    force_ref[...] = result
    for copy in force_copies:
        copy.wait_send()


def body(
    doms,
    grps,
    profile,
    forcing,
    height,
    area,
    stretch,
    face_cell,
    match_owner,
    match_block,
    live_blocks,
    cell_velocity,
):
    blocks, _, points, faces = profile.shape
    rows = 2 * cell_velocity.shape[0]
    everything = pl.BlockSpec(memory_space=pl.ANY)
    vmem = pl.BlockSpec(memory_space=pltpu.VMEM)
    deep = (points, blocks, faces)
    dma = pltpu.SemaphoreType.DMA
    args = (
        profile,
        forcing.astype(F32).reshape(2 * blocks, faces),
        height,
        area,
        stretch.reshape(1, blocks),
        face_cell,
        match_owner,
        match_block,
        live_blocks.reshape(1, -1),
        cell_velocity.reshape(rows, faces),
    )
    shear, force = pl.pallas_call(
        functools.partial(kernel, doms, grps),
        out_shape=(
            jax.ShapeDtypeStruct((2 * blocks, faces), F32),
            jax.ShapeDtypeStruct((rows, faces), F32),
        ),
        in_specs=[everything] * len(args),
        out_specs=(vmem, vmem),
        scratch_shapes=[pltpu.VMEM(arg.shape, arg.dtype) for arg in args[:-1]]
        + [
            pltpu.VMEM((doms, rows, faces), BF16),
            pltpu.VMEM((blocks * 2 * points, faces), F32),
            pltpu.VMEM((points, 2, blocks, faces), F32),
            pltpu.VMEM((points, 2, blocks, faces), F32),
            pltpu.VMEM(deep, F32),
            pltpu.VMEM(deep, F32),
            pltpu.VMEM(deep, F32),
            pltpu.VMEM(deep, F32),
            pltpu.VMEM((blocks, faces, faces), BF16),
            pltpu.VMEM((8 * blocks, faces), F32),
            pltpu.VMEM((doms, rows, faces), F32),
            pltpu.VMEM((doms, rows, faces), F32),
            dma((len(args) - 1,)),
            dma,
            dma((doms,)),
            dma((doms,)),
            dma((doms,)),
            dma((doms,)),
        ],
        compiler_params=pltpu.CompilerParams(collective_id=0, has_side_effects=True),
        name="wall_model",
    )(*args)
    return (
        shear.reshape(blocks, 2, faces),
        force.reshape(cell_velocity.shape[0], 2, faces),
    )


def solution(mesh):
    in_specs = (
        P(("dom", "grp"), None, None, None),
        P(("dom", "grp"), None, None),
        P(("dom", "grp"), None),
        P(("dom", "grp"), None),
        P(("dom", "grp")),
        P(("dom", "grp"), None),
        P(None, "grp", None),
        P(None, "grp", None),
        P(),
        P(("dom", "grp"), None, None),
    )
    out_specs = (P(("dom", "grp"), None, None), P(("dom", "grp"), None, None))
    step = functools.partial(body, mesh.shape["dom"], mesh.shape["grp"])
    return jax.shard_map(step, mesh=mesh, in_specs=in_specs, out_specs=out_specs, check_vma=False)
```

```python
import functools

import jax
import jax.numpy as jnp
from jax import lax
from jax.experimental import pallas as pl
from jax.experimental.pallas import tpu as pltpu
from jax.sharding import PartitionSpec as P

STEPS = 4
VISCOSITY = 0.005
KARMAN = 0.41
TIME_STEP = 2.0
PUSH_GAIN = 0.5
BASE_RATE = 1.5
MESH = pl.DeviceIdType.MESH
F32 = jnp.float32
BF16 = jnp.bfloat16


def kernel(
    doms,
    grps,
    prof_h,
    forc_h,
    height_h,
    area_h,
    stretch_h,
    face_h,
    owner_h,
    target_h,
    live_h,
    cell_h,
    shear_ref,
    force_ref,
    prof,
    forc,
    height,
    area,
    stretch,
    face,
    owner,
    target,
    live,
    table,
    stage,
    u,
    gval,
    fac,
    base,
    quad,
    gap,
    pick,
    cells,
    packed,
    arrived,
    forc32,
    in_sem,
    own_sem,
    cell_send,
    cell_recv,
    force_send,
    force_recv,
):
    blocks, _, points, faces = prof.shape
    rows = cell_h.shape[0]
    me = lax.axis_index("dom")
    mine = lax.axis_index("grp")
    wide = (blocks, faces)

    barrier = pltpu.get_barrier_semaphore()
    for j in range(1, doms):
        pl.semaphore_signal(
            barrier, inc=1, device_id={"dom": lax.rem(me + j, doms)}, device_id_type=MESH
        )
    loads = []
    for i, (src, dst) in enumerate(
        (
            (stretch_h, stretch),
            (height_h, height),
            (owner_h, owner),
            (target_h, target),
            (face_h, face),
            (prof_h, prof),
            (forc_h, forc),
            (area_h, area),
            (live_h, live),
        )
    ):
        loads.append(pltpu.make_async_copy(src, dst, in_sem.at[i]))
        loads[-1].start()
    own = pltpu.make_async_copy(cell_h, table.at[me], own_sem)
    own.start()
    pl.semaphore_wait(barrier, doms - 1)
    cell_copies = []
    for j in range(1, doms):
        cell_copies.append(
            pltpu.make_async_remote_copy(
                src_ref=cell_h,
                dst_ref=table.at[me],
                send_sem=cell_send.at[j],
                recv_sem=cell_recv.at[j],
                device_id={"dom": lax.rem(me + j, doms)},
                device_id_type=MESH,
            )
        )
        cell_copies[-1].start()
    for load in loads:
        load.wait()

    eye = lax.broadcasted_iota(jnp.int32, (blocks, blocks), 0) == lax.broadcasted_iota(
        jnp.int32, (blocks, blocks), 1
    )

    def as_column(row):
        spread = jnp.broadcast_to(row.astype(F32), (blocks, blocks))
        return jnp.sum(jnp.where(eye, spread, 0.0), axis=1, keepdims=True)

    rate = BASE_RATE + as_column(stretch[...])
    tall = height[...].astype(F32)
    step_rate = jnp.broadcast_to(rate / points, wide)
    growth = jnp.exp(step_rate)
    first = (growth - 1.0) / (jnp.exp(jnp.broadcast_to(rate, wide)) - 1.0)
    base_scale = TIME_STEP * VISCOSITY / (first * tall)
    gap_scale = 0.5 * tall * first * (1.0 + growth)
    mid_scale = 1.0 / (growth - 1.0)
    mid_first = 0.5 * (1.0 + growth)

    def grid_level(m, carry):
        level = m.astype(F32)
        shrink = jnp.exp(-step_rate * level)
        base[m] = base_scale * shrink
        ratio = KARMAN * (mid_first - shrink) * mid_scale
        quad[m] = TIME_STEP * ratio * ratio
        gap[m] = gap_scale * jnp.exp(step_rate * (level - 1.0))
        return carry

    lax.fori_loop(0, points, grid_level, 0)

    def widen(b, carry):
        stage[pl.ds(pl.multiple_of(b * 2 * points, 2 * points), 2 * points), :] = (
            prof[b].astype(F32).reshape(2 * points, faces)
        )
        return carry

    lax.fori_loop(0, blocks, widen, 0)

    def turn(k, carry):
        for c in range(2):
            u[k, c] = stage[pl.ds(c * points + k, blocks, stride=2 * points), :]
        return carry

    lax.fori_loop(0, points, turn, 0)

    forc32[...] = forc[...].astype(F32)
    face_now = face[...]
    cell_ids = lax.broadcasted_iota(jnp.int32, (faces, faces), 0)

    for b in range(blocks):
        pick[b] = (cell_ids == face_now[b : b + 1, :]).astype(F32).astype(BF16)

    row_global = owner[me] * rows + 2 * target[me]
    col_global = as_column(row_global).astype(jnp.int32)
    slots = doms * rows
    slot_lane = lax.broadcasted_iota(jnp.int32, (blocks, slots), 1)
    choose = jnp.concatenate(
        [(slot_lane == col_global + c).astype(F32) for c in range(2)], axis=0
    ).astype(BF16)

    own.wait()
    for copy in cell_copies:
        copy.wait()

    held = table[...].astype(F32).reshape(slots, faces).astype(BF16)
    slot_rows = jnp.dot(choose, held, preferred_element_type=F32)
    matching = [
        jnp.take_along_axis(
            slot_rows[c * blocks : (c + 1) * blocks], face_now, axis=1, mode="promise_in_bounds"
        )
        for c in range(2)
    ]
    source = []
    for c in range(2):
        push = forc32[pl.ds(c, blocks, stride=2), :] + matching[c] - u[points - 1, c]
        source.append(TIME_STEP * PUSH_GAIN * push)
        u[points - 1, c] = matching[c]

    def flux(m, low, high):
        d0 = high[0] - low[0]
        d1 = high[1] - low[1]
        square = d0 * d0 + d1 * d1
        root = square * lax.rsqrt(jnp.maximum(square, 1e-37))
        return base[m] + quad[m] * root

    def point(k):
        return (u[k - 1, 0], u[k - 1, 1])

    zero = jnp.zeros(wide, F32)
    half = points // 2

    def eliminate(k, e, g, near, far, here):
        h = gap[k]
        p = h + near * e
        r = 1.0 / (p + far)
        e_new = p * r
        f_new = far * r
        g_new = tuple((h * (here[c] + source[c]) + near * g[c]) * r for c in range(2))
        return e_new, f_new, g_new

    def time_step(_, carry):
        below = point(1)
        low_flux = flux(0, (zero, zero), below)
        low_e, low_g = jnp.ones(wide, F32), (zero, zero)
        above = point(points - 1)
        edge = point(points)
        high_flux = flux(points - 1, above, edge)
        high_e, high_g = jnp.ones(wide, F32), edge
        for i in range(half):
            k = i + 1
            after = point(k + 1)
            next_flux = flux(k, below, after)
            low_e, low_f, low_g = eliminate(k, low_e, low_g, low_flux, next_flux, below)
            if i < half - 1:
                fac[k] = low_f
                for c in range(2):
                    gval[k, c] = low_g[c]
            low_flux, below = next_flux, after
            k = points - 1 - i
            if k > half:
                after = point(k - 1)
                next_flux = flux(k - 1, after, above)
                high_e, high_f, high_g = eliminate(
                    k, high_e, high_g, high_flux, next_flux, above
                )
                if k > half + 1:
                    fac[k] = high_f
                    for c in range(2):
                        gval[k, c] = high_g[c]
                high_flux, above = next_flux, after
        share = 1.0 / (low_e + low_f * high_e)
        down = [(low_g[c] + low_f * high_g[c]) * share for c in range(2)]
        up = [high_g[c] + high_f * down[c] for c in range(2)]
        for c in range(2):
            u[half - 1, c] = down[c]
            u[half, c] = up[c]
        for i in range(1, half):
            k = half - i
            f = fac[k]
            for c in range(2):
                down[c] = gval[k, c] + f * down[c]
                u[k - 1, c] = down[c]
            k = half + 1 + i
            if k < points:
                f = fac[k]
                for c in range(2):
                    up[c] = gval[k, c] + f * up[c]
                    u[k - 1, c] = up[c]
        return carry

    lax.fori_loop(0, STEPS, time_step, 0)

    wall = point(1)
    wall_flux = flux(0, (zero, zero), wall) * (1.0 / TIME_STEP)
    lane = lax.broadcasted_iota(jnp.int32, live.shape, 1)
    own_live = jnp.sum(
        jnp.where(lane == me * grps + mine, live[...], 0).astype(F32), axis=1, keepdims=True
    )
    alive = lax.broadcasted_iota(jnp.int32, wide, 0).astype(F32) < own_live
    size = area[...]
    pieces = []
    for c in range(2):
        shear = jnp.where(alive, wall_flux * wall[c], 0.0)
        shear_ref[pl.ds(c, blocks, stride=2), :] = shear
        pieces.append(shear * size)
    for c in range(2):
        top = pieces[c].astype(BF16).astype(F32)
        cells[pl.ds(c, blocks, stride=8), :] = top
        cells[pl.ds(2 + c, blocks, stride=8), :] = pieces[c] - top
    for c in range(4):
        cells[pl.ds(4 + c, blocks, stride=8), :] = zero
    for b in range(blocks):
        part = cells[pl.ds(8 * b, 8), :].astype(BF16)
        cells[pl.ds(8 * b, 8), :] = lax.dot_general(
            part, pick[b], (((1,), (1,)), ((), ())), preferred_element_type=F32
        )
    slot_row = lax.broadcasted_iota(jnp.int32, (slots, blocks), 0)
    total = jnp.zeros((slots, faces), F32)
    for c in range(2):
        by_cell = cells[pl.ds(c, blocks, stride=8), :] + cells[pl.ds(2 + c, blocks, stride=8), :]
        place = (slot_row == row_global + c).astype(F32)
        total += jnp.dot(
            place, by_cell, precision=lax.Precision.HIGHEST, preferred_element_type=F32
        )
    packed[...] = total.reshape(doms, rows, faces)
    force_copies = []
    for j in range(1, doms):
        peer = lax.rem(me + j, doms)
        force_copies.append(
            pltpu.make_async_remote_copy(
                src_ref=packed.at[peer],
                dst_ref=arrived.at[j],
                send_sem=force_send.at[j],
                recv_sem=force_recv.at[j],
                device_id={"dom": peer},
                device_id_type=MESH,
            )
        )
        force_copies[-1].start()
    result = packed[me]
    for j in range(1, doms):
        force_copies[j - 1].wait_recv()
        result += arrived[j]
    force_ref[...] = result
    for copy in force_copies:
        copy.wait_send()


def body(
    doms,
    grps,
    profile,
    forcing,
    height,
    area,
    stretch,
    face_cell,
    match_owner,
    match_block,
    live_blocks,
    cell_velocity,
):
    blocks, _, points, faces = profile.shape
    rows = 2 * cell_velocity.shape[0]
    everything = pl.BlockSpec(memory_space=pltpu.HBM)
    vmem = pl.BlockSpec(memory_space=pltpu.VMEM)
    deep = (points, blocks, faces)
    dma = pltpu.SemaphoreType.DMA
    vmem_bytes = 32 << 20
    args = (
        profile,
        forcing.reshape(2 * blocks, faces),
        height,
        area,
        stretch.reshape(1, blocks),
        face_cell,
        match_owner,
        match_block,
        live_blocks.reshape(1, -1),
        cell_velocity.reshape(rows, faces),
    )
    shear, force = pl.pallas_call(
        functools.partial(kernel, doms, grps),
        out_shape=(
            jax.ShapeDtypeStruct((2 * blocks, faces), F32),
            jax.ShapeDtypeStruct((rows, faces), F32),
        ),
        in_specs=[everything] * len(args),
        out_specs=(vmem, vmem),
        scratch_shapes=[pltpu.VMEM(arg.shape, arg.dtype) for arg in args[:-1]]
        + [
            pltpu.VMEM((doms, rows, faces), BF16),
            pltpu.VMEM((blocks * 2 * points, faces), F32),
            pltpu.VMEM((points, 2, blocks, faces), F32),
            pltpu.VMEM((points, 2, blocks, faces), F32),
            pltpu.VMEM(deep, F32),
            pltpu.VMEM(deep, F32),
            pltpu.VMEM(deep, F32),
            pltpu.VMEM(deep, F32),
            pltpu.VMEM((blocks, faces, faces), BF16),
            pltpu.VMEM((8 * blocks, faces), F32),
            pltpu.VMEM((doms, rows, faces), F32),
            pltpu.VMEM((doms, rows, faces), F32),
            pltpu.VMEM((2 * blocks, faces), F32),
            dma((len(args) - 1,)),
            dma,
            dma((doms,)),
            dma((doms,)),
            dma((doms,)),
            dma((doms,)),
        ],
        compiler_params=pltpu.CompilerParams(
            collective_id=0, has_side_effects=True, vmem_limit_bytes=vmem_bytes
        ),
        name="wall_model",
    )(*[pltpu.with_memory_space_constraint(x, pltpu.HBM) for x in args])
    return (
        shear.reshape(blocks, 2, faces),
        force.reshape(cell_velocity.shape[0], 2, faces),
    )


def solution(mesh):
    in_specs = (
        P(("dom", "grp"), None, None, None),
        P(("dom", "grp"), None, None),
        P(("dom", "grp"), None),
        P(("dom", "grp"), None),
        P(("dom", "grp")),
        P(("dom", "grp"), None),
        P(None, "grp", None),
        P(None, "grp", None),
        P(),
        P(("dom", "grp"), None, None),
    )
    out_specs = (P(("dom", "grp"), None, None), P(("dom", "grp"), None, None))
    step = functools.partial(body, mesh.shape["dom"], mesh.shape["grp"])
    return jax.shard_map(step, mesh=mesh, in_specs=in_specs, out_specs=out_specs, check_vma=False)
```

```python
import functools

import jax
import jax.numpy as jnp
from jax import lax
from jax.experimental import pallas as pl
from jax.experimental.pallas import tpu as pltpu
from jax.sharding import PartitionSpec as P

STEPS = 4
VISCOSITY = 0.005
KARMAN = 0.41
TIME_STEP = 2.0
PUSH_GAIN = 0.5
BASE_RATE = 1.5
MESH = pl.DeviceIdType.MESH
F32 = jnp.float32
BF16 = jnp.bfloat16


def kernel(
    doms,
    grps,
    prof_h,
    forc_h,
    height_h,
    area_h,
    stretch_h,
    face_h,
    owner_h,
    target_h,
    live_h,
    cell_h,
    shear_ref,
    force_ref,
    prof,
    forc,
    height,
    area,
    stretch,
    face,
    owner,
    target,
    live,
    table,
    stage,
    u,
    gval,
    fac,
    base,
    quad,
    gap,
    pick,
    cells,
    packed,
    arrived,
    forc32,
    in_sem,
    own_sem,
    cell_send,
    cell_recv,
    force_send,
    force_recv,
):
    blocks, _, points, faces = prof.shape
    rows = cell_h.shape[0]
    me = lax.axis_index("dom")
    mine = lax.axis_index("grp")
    wide = (blocks, faces)

    barrier = pltpu.get_barrier_semaphore()
    for j in range(1, doms):
        pl.semaphore_signal(
            barrier, inc=1, device_id={"dom": lax.rem(me + j, doms)}, device_id_type=MESH
        )
    loads = []
    for i, (src, dst) in enumerate(
        (
            (stretch_h, stretch),
            (height_h, height),
            (owner_h, owner),
            (target_h, target),
            (face_h, face),
            (prof_h, prof),
            (forc_h, forc),
            (area_h, area),
            (live_h, live),
        )
    ):
        loads.append(pltpu.make_async_copy(src, dst, in_sem.at[i]))
        loads[-1].start()
    own = pltpu.make_async_copy(cell_h, table.at[me], own_sem)
    own.start()
    pl.semaphore_wait(barrier, doms - 1)
    cell_copies = []
    for j in range(1, doms):
        cell_copies.append(
            pltpu.make_async_remote_copy(
                src_ref=cell_h,
                dst_ref=table.at[me],
                send_sem=cell_send.at[j],
                recv_sem=cell_recv.at[j],
                device_id={"dom": lax.rem(me + j, doms)},
                device_id_type=MESH,
            )
        )
        cell_copies[-1].start()
    for load in loads:
        load.wait()

    eye = lax.broadcasted_iota(jnp.int32, (blocks, blocks), 0) == lax.broadcasted_iota(
        jnp.int32, (blocks, blocks), 1
    )

    def as_column(row):
        spread = jnp.broadcast_to(row.astype(F32), (blocks, blocks))
        return jnp.sum(jnp.where(eye, spread, 0.0), axis=1, keepdims=True)

    rate = BASE_RATE + as_column(stretch[...])
    tall = height[...].astype(F32)
    step_rate = jnp.broadcast_to(rate / points, wide)
    growth = jnp.exp(step_rate)
    first = (growth - 1.0) / (jnp.exp(jnp.broadcast_to(rate, wide)) - 1.0)
    base_scale = TIME_STEP * VISCOSITY / (first * tall)
    gap_scale = 0.5 * tall * first * (1.0 + growth)
    mid_scale = 1.0 / (growth - 1.0)
    mid_first = 0.5 * (1.0 + growth)

    def grid_level(m, carry):
        level = m.astype(F32)
        shrink = jnp.exp(-step_rate * level)
        base[m] = base_scale * shrink
        ratio = KARMAN * (mid_first - shrink) * mid_scale
        quad[m] = TIME_STEP * ratio * ratio
        gap[m] = gap_scale * jnp.exp(step_rate * (level - 1.0))
        return carry

    lax.fori_loop(0, points, grid_level, 0)

    def widen(b, carry):
        stage[pl.ds(pl.multiple_of(b * 2 * points, 2 * points), 2 * points), :] = (
            prof[b].astype(F32).reshape(2 * points, faces)
        )
        return carry

    lax.fori_loop(0, blocks, widen, 0)

    def turn(k, carry):
        for c in range(2):
            u[k, c] = stage[pl.ds(c * points + k, blocks, stride=2 * points), :]
        return carry

    lax.fori_loop(0, points, turn, 0)

    forc32[...] = forc[...].astype(F32)
    face_now = face[...]
    cell_ids = lax.broadcasted_iota(jnp.int32, (faces, faces), 0)

    for b in range(blocks):
        pick[b] = (cell_ids == face_now[b : b + 1, :]).astype(F32).astype(BF16)

    row_global = owner[me] * rows + 2 * target[me]
    col_global = as_column(row_global).astype(jnp.int32)
    slots = doms * rows
    slot_lane = lax.broadcasted_iota(jnp.int32, (blocks, slots), 1)
    choose = jnp.concatenate(
        [(slot_lane == col_global + c).astype(F32) for c in range(2)], axis=0
    ).astype(BF16)

    own.wait()
    for copy in cell_copies:
        copy.wait()

    held = table[...].astype(F32).reshape(slots, faces).astype(BF16)
    slot_rows = jnp.dot(choose, held, preferred_element_type=F32)
    matching = [
        jnp.take_along_axis(
            slot_rows[c * blocks : (c + 1) * blocks], face_now, axis=1, mode="promise_in_bounds"
        )
        for c in range(2)
    ]
    source = []
    for c in range(2):
        push = forc32[pl.ds(c, blocks, stride=2), :] + matching[c] - u[points - 1, c]
        source.append(TIME_STEP * PUSH_GAIN * push)
        u[points - 1, c] = matching[c]

    def flux(m, low, high):
        d0 = high[0] - low[0]
        d1 = high[1] - low[1]
        square = d0 * d0 + d1 * d1
        root = square * lax.rsqrt(jnp.maximum(square, 1e-37))
        return base[m] + quad[m] * root

    def point(k):
        return (u[k - 1, 0], u[k - 1, 1])

    zero = jnp.zeros(wide, F32)
    half = points // 2

    def eliminate(k, e, g, near, far, here):
        h = gap[k]
        p = h + near * e
        r = 1.0 / (p + far)
        e_new = p * r
        f_new = far * r
        g_new = tuple((h * (here[c] + source[c]) + near * g[c]) * r for c in range(2))
        return e_new, f_new, g_new

    def time_step(_, carry):
        below = point(1)
        low_flux = flux(0, (zero, zero), below)
        low_e, low_g = jnp.ones(wide, F32), (zero, zero)
        above = point(points - 1)
        edge = point(points)
        high_flux = flux(points - 1, above, edge)
        high_e, high_g = jnp.ones(wide, F32), edge
        for i in range(half):
            k = i + 1
            after = point(k + 1)
            next_flux = flux(k, below, after)
            low_e, low_f, low_g = eliminate(k, low_e, low_g, low_flux, next_flux, below)
            if i < half - 1:
                fac[k] = low_f
                for c in range(2):
                    gval[k, c] = low_g[c]
            low_flux, below = next_flux, after
            k = points - 1 - i
            if k > half:
                after = point(k - 1)
                next_flux = flux(k - 1, after, above)
                high_e, high_f, high_g = eliminate(
                    k, high_e, high_g, high_flux, next_flux, above
                )
                if k > half + 1:
                    fac[k] = high_f
                    for c in range(2):
                        gval[k, c] = high_g[c]
                high_flux, above = next_flux, after
        share = 1.0 / (low_e + low_f * high_e)
        down = [(low_g[c] + low_f * high_g[c]) * share for c in range(2)]
        up = [high_g[c] + high_f * down[c] for c in range(2)]
        for c in range(2):
            u[half - 1, c] = down[c]
            u[half, c] = up[c]
        for i in range(1, half):
            k = half - i
            f = fac[k]
            for c in range(2):
                down[c] = gval[k, c] + f * down[c]
                u[k - 1, c] = down[c]
            k = half + 1 + i
            if k < points:
                f = fac[k]
                for c in range(2):
                    up[c] = gval[k, c] + f * up[c]
                    u[k - 1, c] = up[c]
        return carry

    lax.fori_loop(0, STEPS, time_step, 0)

    wall = point(1)
    wall_flux = flux(0, (zero, zero), wall) * (1.0 / TIME_STEP)
    lane = lax.broadcasted_iota(jnp.int32, live.shape, 1)
    own_live = jnp.sum(
        jnp.where(lane == me * grps + mine, live[...], 0).astype(F32), axis=1, keepdims=True
    )
    alive = lax.broadcasted_iota(jnp.int32, wide, 0).astype(F32) < own_live
    size = area[...]
    pieces = []
    for c in range(2):
        shear = jnp.where(alive, wall_flux * wall[c], 0.0)
        shear_ref[pl.ds(c, blocks, stride=2), :] = shear
        pieces.append(shear * size)
    for c in range(2):
        top = pieces[c].astype(BF16).astype(F32)
        cells[pl.ds(c, blocks, stride=8), :] = top
        cells[pl.ds(2 + c, blocks, stride=8), :] = pieces[c] - top
    for c in range(4):
        cells[pl.ds(4 + c, blocks, stride=8), :] = zero
    for b in range(blocks):
        part = cells[pl.ds(8 * b, 8), :].astype(BF16)
        cells[pl.ds(8 * b, 8), :] = lax.dot_general(
            part, pick[b], (((1,), (1,)), ((), ())), preferred_element_type=F32
        )
    slot_row = lax.broadcasted_iota(jnp.int32, (slots, blocks), 0)
    places, terms = [], []
    for c in range(2):
        by_cell = cells[pl.ds(c, blocks, stride=8), :] + cells[pl.ds(2 + c, blocks, stride=8), :]
        place = (slot_row == row_global + c).astype(F32)
        top = by_cell.astype(BF16).astype(F32)
        places += [place, place]
        terms += [top, by_cell - top]
    total = jnp.dot(
        jnp.concatenate(places, axis=1).astype(BF16),
        jnp.concatenate(terms, axis=0).astype(BF16),
        preferred_element_type=F32,
    )
    packed[...] = total.reshape(doms, rows, faces)
    force_copies = []
    for j in range(1, doms):
        peer = lax.rem(me + j, doms)
        force_copies.append(
            pltpu.make_async_remote_copy(
                src_ref=packed.at[peer],
                dst_ref=arrived.at[j],
                send_sem=force_send.at[j],
                recv_sem=force_recv.at[j],
                device_id={"dom": peer},
                device_id_type=MESH,
            )
        )
        force_copies[-1].start()
    result = packed[me]
    for j in range(1, doms):
        force_copies[j - 1].wait_recv()
        result += arrived[j]
    force_ref[...] = result
    for copy in force_copies:
        copy.wait_send()


def emit(shear_ref, force_ref, shear_out, force_out, sem):
    copies = (
        pltpu.make_async_copy(shear_ref, shear_out, sem.at[0]),
        pltpu.make_async_copy(force_ref, force_out, sem.at[1]),
    )
    for copy in copies:
        copy.start()
    for copy in copies:
        copy.wait()


def body(
    doms,
    grps,
    profile,
    forcing,
    height,
    area,
    stretch,
    face_cell,
    match_owner,
    match_block,
    live_blocks,
    cell_velocity,
):
    blocks, _, points, faces = profile.shape
    rows = 2 * cell_velocity.shape[0]
    everything = pl.BlockSpec(memory_space=pltpu.HBM)
    vmem = pl.BlockSpec(memory_space=pltpu.VMEM)
    deep = (points, blocks, faces)
    dma = pltpu.SemaphoreType.DMA
    vmem_bytes = 32 << 20
    args = (
        profile,
        forcing.reshape(2 * blocks, faces),
        height,
        area,
        stretch.reshape(1, blocks),
        face_cell,
        match_owner,
        match_block,
        live_blocks.reshape(1, -1),
        cell_velocity.reshape(rows, faces),
    )
    shear, force = pl.pallas_call(
        functools.partial(kernel, doms, grps),
        out_shape=(
            jax.ShapeDtypeStruct((2 * blocks, faces), F32),
            jax.ShapeDtypeStruct((rows, faces), F32),
        ),
        in_specs=[everything] * len(args),
        out_specs=(vmem, vmem),
        scratch_shapes=[pltpu.VMEM(arg.shape, arg.dtype) for arg in args[:-1]]
        + [
            pltpu.VMEM((doms, rows, faces), BF16),
            pltpu.VMEM((blocks * 2 * points, faces), F32),
            pltpu.VMEM((points, 2, blocks, faces), F32),
            pltpu.VMEM((points, 2, blocks, faces), F32),
            pltpu.VMEM(deep, F32),
            pltpu.VMEM(deep, F32),
            pltpu.VMEM(deep, F32),
            pltpu.VMEM(deep, F32),
            pltpu.VMEM((blocks, faces, faces), BF16),
            pltpu.VMEM((8 * blocks, faces), F32),
            pltpu.VMEM((doms, rows, faces), F32),
            pltpu.VMEM((doms, rows, faces), F32),
            pltpu.VMEM((2 * blocks, faces), F32),
            dma((len(args) - 1,)),
            dma,
            dma((doms,)),
            dma((doms,)),
            dma((doms,)),
            dma((doms,)),
        ],
        compiler_params=pltpu.CompilerParams(
            collective_id=0, has_side_effects=True, vmem_limit_bytes=vmem_bytes
        ),
        name="wall_model",
    )(*[pltpu.with_memory_space_constraint(x, pltpu.HBM) for x in args])
    shear, force = pl.pallas_call(
        emit,
        out_shape=(
            jax.ShapeDtypeStruct(shear.shape, F32),
            jax.ShapeDtypeStruct(force.shape, F32),
        ),
        in_specs=[pl.BlockSpec(memory_space=pl.ANY)] * 2,
        out_specs=(pl.BlockSpec(memory_space=pl.ANY),) * 2,
        scratch_shapes=[dma((2,))],
        compiler_params=pltpu.CompilerParams(vmem_limit_bytes=1 << 20),
        name="emit",
    )(shear, force)
    return (
        shear.reshape(blocks, 2, faces),
        force.reshape(cell_velocity.shape[0], 2, faces),
    )


def solution(mesh):
    in_specs = (
        P(("dom", "grp"), None, None, None),
        P(("dom", "grp"), None, None),
        P(("dom", "grp"), None),
        P(("dom", "grp"), None),
        P(("dom", "grp")),
        P(("dom", "grp"), None),
        P(None, "grp", None),
        P(None, "grp", None),
        P(),
        P(("dom", "grp"), None, None),
    )
    out_specs = (P(("dom", "grp"), None, None), P(("dom", "grp"), None, None))
    step = functools.partial(body, mesh.shape["dom"], mesh.shape["grp"])
    return jax.shard_map(step, mesh=mesh, in_specs=in_specs, out_specs=out_specs, check_vma=False)
```
